32 devices in a mesh: groups: 2 (over x), tensor: 16 (over z, y, core).
Axes of the slice: x: 2, y: 2, z: 4, core: 2. Of those that a mesh axis runs over, the one named last changes fastest.
Arguments:
- tokens: bfloat16 [1024, 8192], P('groups', 'tensor'), parts along dimension 0, may hold values from -6 to 6
- norm_gain: float32 [8192], P('tensor'), may hold values from 0.1 to 1.9
- w_in: bfloat16 [8192, 3, 8192], P(None, None, 'tensor'), may hold values from -0.0625 to 0.0625
- w_short: float32 [3, 3, 8192], P(None, None, 'tensor'), may hold values from -3 to 3
- filters: bfloat16 [512, 128], P('tensor'), may hold values from -0.5 to 0.5
- skip: float32 [8192], P('tensor'), may hold values from -4 to 4
- w_out: bfloat16 [8192, 8192], P('tensor'), may hold values from -0.0625 to 0.0625
Outputs:
- mixed: bfloat16 [1024, 8192], P('groups', 'tensor'), parts along dimension 0
The draws below stay inside these ranges and needn't reach their ends.
There are 2 independent parts, one for each index of `groups`. The reference program is written for one: setup_inputs(seed, part) draws one part's arguments, and reference() takes and returns one part's arrays. A program takes and returns all parts, laid end to end along the dimension named above; an argument that names none is the same for every part. Nothing has to cross between parts.
All inputs are finite; a program needn't handle non-finite values.
Results may differ from the reference program's by a relative error of at most 0.0085.
Values may be sent and summed in bfloat16 or wider, within the bound.
A program may use at most 192 MiB of HBM per device.

```python
import jax
import jax.numpy as jnp
from jax import lax

D = 8192
TAPS = 128
GROUP = 16
SHORT = 3
TOKENS = 512
FILTERS = 512


def draw_tokens(key, part):
    column = jnp.arange(D, dtype=jnp.float32) / (D - 1)
    scale = 0.5 * jnp.exp(jnp.log(3.0) * column)
    base = jax.random.truncated_normal(key, -4.0, 4.0, (TOKENS, D), jnp.float32)
    return (base * scale[None, :]).astype(jnp.bfloat16)


def shard_levels(rng, dims, shards, least, largest):
    level, own = 1.0, jax.random.fold_in(rng, 6)
    for position, parts in shards:
        steps = jnp.exp(jax.random.uniform(jax.random.fold_in(own, position), (parts,), jnp.float32, least / len(shards), largest / len(shards)))
        level = level * jnp.repeat(steps, dims[position] // parts).reshape([-1 if axis == position else 1 for axis in range(len(dims))])
    return level


def normal_values(key, shape, width, reach, split=(), kind=jnp.bfloat16):
    values = width * jax.random.normal(key, shape, jnp.float32)
    if split:
        values = values * shard_levels(key, shape, split, -0.22, 0.18)
    return jnp.clip(values, -reach, reach).astype(kind)


def setup_inputs(seed: int = 0, part: int = 0) -> dict:
    splits = jax.random.split(jax.random.key(seed), 8)
    part_keys = jax.random.split(jax.random.fold_in(splits[7], part), 8)
    return {
        "tokens": draw_tokens(jax.random.fold_in(jax.random.fold_in(splits[7], part), 71), part),
        "norm_gain": jnp.clip(1.0 + 0.18 * jax.random.normal(splits[1], (D,), jnp.float32), 0.1, 1.9),
        "w_in": normal_values(splits[2], (D, 3, D), D ** -0.5, 0.0625, ((2, 16),)),
        "w_short": normal_values(splits[3], (SHORT, 3, D), 0.6, 3.0, ((2, 16),), jnp.float32),
        "filters": normal_values(splits[4], (FILTERS, TAPS), 0.09, 0.5, ((0, 16),)),
        "skip": normal_values(splits[5], (D,), 1.0, 4.0, ((0, 16),), jnp.float32),
        "w_out": normal_values(splits[6], (D, D), D ** -0.5, 0.0625, ((0, 16),)),
    }


def shifted(field, lag):
    pads = ((lag, 0),) + ((0, 0),) * (field.ndim - 1)
    return jnp.pad(field, pads)[:field.shape[0]]

def reference(tokens, norm_gain, w_in, w_short, filters, skip, w_out):
    wide = tokens.astype(jnp.float32)
    factor = lax.rsqrt(lax.optimization_barrier(jnp.mean(wide * wide, axis=1, keepdims=True)) + 1e-05)
    normed = (wide * factor * norm_gain[None, :]).astype(jnp.bfloat16)
    proj = jnp.dot(normed, w_in.reshape(D, 3 * D), preferred_element_type=jnp.float32)
    proj = proj.reshape(TOKENS, 3, D)
    short = w_short[0][None] * proj
    for lag in range(1, SHORT):
        short = short + w_short[lag][None] * shifted(proj, lag)
    gated = (short[:, 1] * short[:, 2]).astype(jnp.bfloat16)
    gated_wide = gated.astype(jnp.float32)
    taps_wide = jnp.repeat(filters.astype(jnp.float32), GROUP, axis=0)
    padded = jnp.pad(gated_wide, ((TAPS, 0), (0, 0)))

    def add_tap(step, total):
        step = step.astype(jnp.int32)
        window = lax.dynamic_slice_in_dim(padded, (TAPS - step).astype(jnp.int32), TOKENS, 0)
        column = lax.dynamic_index_in_dim(taps_wide, step, 1, keepdims=False)
        return total + column[None, :] * window
    conv = lax.fori_loop(0, TAPS, add_tap, jnp.zeros((TOKENS, D), jnp.float32))
    hidden = ((conv + skip[None, :] * gated_wide) * short[:, 0]).astype(jnp.bfloat16)
    result = wide + jnp.dot(hidden, w_out, preferred_element_type=jnp.float32)
    return result.astype(jnp.bfloat16)
```

```python
import functools

import jax
import jax.numpy as jnp
from jax import lax
from jax.experimental import pallas as pl
from jax.experimental.pallas import tpu as pltpu
from jax.sharding import PartitionSpec as P

MESH = pl.DeviceIdType.MESH
LANES = 128
PIECES = 2


def chip_at(pos, m):
    upper = pos // (m // 2)
    return (1 - upper) * 2 * pos + upper * (2 * (m - 1 - pos) + 1)


def position_of(chip, m):
    odd = chip % 2
    return (1 - odd) * (chip // 2) + odd * (m - 1 - chip // 2)


class Ring:
    def __init__(self, m):
        me = lax.axis_index("tensor")
        self.m = m
        self.core = me % 2
        self.chip = me // 2
        self.pos = position_of(self.chip, m)
        self.next = (
            {"tensor": chip_at((self.pos + 1) % m, m) * 2 + self.core},
            {"tensor": chip_at((self.pos + m - 1) % m, m) * 2 + self.core},
        )
        self.sibling = {"tensor": self.chip * 2 + 1 - self.core}

    def behind(self, side, steps):
        if side == 0:
            return (self.pos + self.m - steps) % self.m
        return (self.pos + steps) % self.m

    def greet(self):
        barrier = pltpu.get_barrier_semaphore()
        for device in self.next + (self.sibling,):
            pl.semaphore_signal(barrier, inc=1, device_id=device, device_id_type=MESH)

    def met(self):
        pl.semaphore_wait(pltpu.get_barrier_semaphore(), 3)


def remote(src, dst, send, recv, device):
    return pltpu.make_async_remote_copy(
        src_ref=src, dst_ref=dst, send_sem=send, recv_sem=recv,
        device_id=device, device_id_type=MESH,
    )


def gather_kernel(
    m, tokens, gain, w_in, w_out, acc, pair,
    xg, wv, w_sem, ring_send, ring_recv, sib_send, sib_recv, own_send, own_recv,
    keep_sem, give_send, give_recv,
):
    rows, width = tokens.shape
    half = rows // 2
    piece = half // PIECES
    ring = Ring(m)
    core = ring.core
    ring.greet()

    def w_copy(d):
        base = pl.multiple_of(chip_at((ring.pos + d) % m, m) * 2 * width, 2 * width)
        part = pl.ds(base, 2 * width)
        return pltpu.make_async_copy(w_in.at[:, part, :], wv.at[:, part, :], w_sem.at[d])

    w_copy(0).start()
    xg[ring.pos, core] = (tokens[...].astype(jnp.float32) * gain[...]).astype(jnp.bfloat16)
    ring.met()

    def span(side, k):
        return pl.ds(side * half + k * piece, piece)

    def hop(s, side, k, q):
        block = xg.at[q, core, span(side, k), :]
        return remote(block, block, ring_send.at[s, side, k], ring_recv.at[s, side, k], ring.next[side])

    def across(s, side, k, q):
        block = xg.at[q, core, span(side, k), :]
        return remote(block, block, sib_send.at[s, side, k], sib_recv.at[s, side, k], ring.sibling)

    def across_in(s, side, k, q):
        block = xg.at[q, 1 - core, span(side, k), :]
        return remote(block, block, sib_send.at[s, side, k], sib_recv.at[s, side, k], ring.sibling)

    for k in range(PIECES):
        for side in range(2):
            hop(0, side, k, ring.pos).start()
    own = remote(xg.at[ring.pos, core], xg.at[ring.pos, core], own_send, own_recv, ring.sibling)
    own.start()
    own_in = remote(xg.at[ring.pos, 1 - core], xg.at[ring.pos, 1 - core], own_send, own_recv, ring.sibling)
    for d in range(1, m // 2 + 1):
        w_copy(d).start()
        if d < m - d:
            w_copy(m - d).start()

    def keep(q):
        base = pl.multiple_of((chip_at(q, m) * 2 + core) * width, width)
        slot = pl.ds(pl.multiple_of(core * width, width), width)
        return pltpu.make_async_copy(w_out.at[:, pl.ds(base, width)], pair.at[q, slot, :], keep_sem.at[q])

    def give(q):
        base = pl.multiple_of((chip_at(q, m) * 2 + 1 - core) * width, width)
        slot = pl.ds(pl.multiple_of(core * width, width), width)
        return remote(w_out.at[:, pl.ds(base, width)], pair.at[q, slot, :], give_send.at[q], give_recv.at[q], ring.sibling)

    def multiply(s, first):
        for side in range(2):
            q = ring.behind(side, s)
            span_rows = pl.ds(side * half, half)
            base = pl.multiple_of(chip_at(q, m) * 2 * width, 2 * width)
            for b in range(3):
                term = jnp.dot(
                    xg[q, 0, span_rows, :], wv[b, pl.ds(base, width), :],
                    preferred_element_type=jnp.float32,
                ) + jnp.dot(
                    xg[q, 1, span_rows, :], wv[b, pl.ds(base + width, width), :],
                    preferred_element_type=jnp.float32,
                )
                if first:
                    acc[b, span_rows, :] = term
                else:
                    acc[b, span_rows, :] += term

    def pass_on(s, last):
        for k in range(PIECES):
            for side in range(2):
                q = ring.behind(side, s + 1)
                hop(s, side, k, q).wait_recv()
                if not last:
                    hop(s + 1, side, k, q).start()
                across(s, side, k, q).start()

    def use(s):
        @pl.when(s <= m // 2)
        def _():
            w_copy(s).wait()

        @pl.when(s < m // 2)
        def _():
            w_copy(m - s).wait()

        for k in range(PIECES):
            for side in range(2):
                across_in(s - 1, side, k, ring.behind(side, s)).wait_recv()
        multiply(s, False)

    w_copy(0).wait()
    own_in.wait_recv()
    multiply(0, True)
    pass_on(0, m == 2)

    def body(s, carry):
        keep(s - 1).start()
        give(s - 1).start()
        use(s)
        pass_on(s, False)
        return carry

    lax.fori_loop(1, m - 2, body, 0)
    for q in range(m - 3, m):
        keep(q).start()
        give(q).start()
    use(m - 2)
    pass_on(m - 2, True)
    use(m - 1)

    own.wait_send()

    def settle(s, carry):
        for k in range(PIECES):
            for side in range(2):
                hop(s, side, k, ring.behind(side, s)).wait_send()
                across(s, side, k, ring.behind(side, s + 1)).wait_send()
        return carry

    lax.fori_loop(0, m - 1, settle, 0)

    def settle_pairs(q, carry):
        keep(q).wait()
        give(q).wait_send()
        slot = pl.ds(pl.multiple_of((1 - core) * width, width), width)
        view = pair.at[q, slot, :]
        remote(view, view, give_send.at[q], give_recv.at[q], ring.sibling).wait_recv()
        return carry

    lax.fori_loop(0, m, settle_pairs, 0)


def scatter_kernel(
    m, taps, group, proj, factor, w_short, line, skip, pair, tokens, out,
    wv, hid, gs, toep, stage, got, w_sem, ring_send, ring_recv, sib_send, sib_recv,
):
    rows, width = tokens.shape
    half = rows // 2
    piece = half // PIECES
    window = 2 * taps
    per_tile = LANES // group
    ring = Ring(m)
    core = ring.core
    ring.greet()
    fetch = pltpu.make_async_copy(pair, wv, w_sem)
    fetch.start()
    gs[0:taps, :] = jnp.zeros((taps, LANES), jnp.bfloat16)
    ring.met()

    def across(j, which):
        view = hid.at[which, :, pl.ds(pl.multiple_of(j * LANES, LANES), LANES)]
        return remote(view, view, sib_send.at[j], sib_recv.at[j], ring.sibling)

    def tile(j, carry):
        lanes = pl.ds(pl.multiple_of(j * LANES, LANES), LANES)
        at_row = lax.broadcasted_iota(jnp.int32, (rows, LANES), 0)

        def short(b):
            x = proj[b, :, lanes] * factor[...]
            total = w_short[0, pl.ds(b, 1), lanes] * x
            for lag in range(1, w_short.shape[0]):
                moved = jnp.where(at_row >= lag, pltpu.roll(x, lag, 0), 0.0)
                total = total + w_short[lag, pl.ds(b, 1), lanes] * moved
            return total

        gs[taps:, :] = (short(1) * short(2)).astype(jnp.bfloat16)
        query = short(0)
        lines = line[pl.ds(pl.multiple_of(j * per_tile, per_tile), per_tile), :]
        for f in range(per_tile):
            spread = jnp.broadcast_to(lines[f : f + 1, :], (taps, window))
            toep[f * taps : (f + 1) * taps, :] = pltpu.roll(
                spread, 0, 1, stride=1, stride_axis=0
            ).astype(jnp.bfloat16)
        owner = lax.broadcasted_iota(jnp.int32, (taps, LANES), 1) // group
        for i in range(rows // taps):
            every = jnp.dot(
                toep[...], gs[i * taps : i * taps + window, :], preferred_element_type=jnp.float32
            )
            conv = every[0:taps]
            for f in range(1, per_tile):
                conv = jnp.where(owner == f, every[f * taps : (f + 1) * taps], conv)
            gated = gs[(i + 1) * taps : (i + 2) * taps, :].astype(jnp.float32)
            part = (conv + skip[:, lanes] * gated) * query[i * taps : (i + 1) * taps]
            hid[core, i * taps : (i + 1) * taps, lanes] = part.astype(jnp.bfloat16)
        across(j, core).start()
        return carry

    tiles = width // LANES
    lax.fori_loop(0, tiles, tile, 0)
    fetch.wait()
    for j in range(tiles):
        across(j, 1 - core).wait_recv()

    def span(k):
        return pl.ds(k * piece, piece)

    def hop(s, side, k):
        return remote(
            stage.at[side, s, span(k), :], got.at[side, s, span(k), :],
            ring_send.at[s, side, k], ring_recv.at[s, side, k], ring.next[side],
        )

    def partial(side, k, q):
        here = pl.ds(side * half + k * piece, piece)
        return jnp.dot(
            hid[0, here, :], wv[q, 0:width, :], preferred_element_type=jnp.float32
        ) + jnp.dot(
            hid[1, here, :], wv[q, width : 2 * width, :], preferred_element_type=jnp.float32
        )

    for k in range(PIECES):
        for side in range(2):
            stage[side, 0, span(k), :] = partial(side, k, ring.behind(side, 1)).astype(jnp.bfloat16)
            hop(0, side, k).start()

    def body(s, carry):
        for k in range(PIECES):
            for side in range(2):
                part = partial(side, k, ring.behind(side, s + 1))
                hop(s - 1, side, k).wait_recv()
                part = part + got[side, s - 1, span(k), :].astype(jnp.float32)
                stage[side, s, span(k), :] = part.astype(jnp.bfloat16)
                hop(s, side, k).start()
        return carry

    lax.fori_loop(1, m - 1, body, 0)
    for k in range(PIECES):
        for side in range(2):
            here = pl.ds(side * half + k * piece, piece)
            part = tokens[here, :].astype(jnp.float32) + partial(side, k, ring.pos)
            hop(m - 2, side, k).wait_recv()
            part = part + got[side, m - 2, span(k), :].astype(jnp.float32)
            out[here, :] = part.astype(jnp.bfloat16)

    def settle(s, carry):
        for k in range(PIECES):
            for side in range(2):
                hop(s, side, k).wait_send()
        return carry

    lax.fori_loop(0, m - 1, settle, 0)
    for j in range(tiles):
        across(j, core).wait_send()


def on_device(n, tokens, norm_gain, w_in, w_short, filters, skip, w_out):
    m = n // 2
    rows, width = tokens.shape
    depth = w_in.shape[0]
    count, taps = filters.shape
    group = width // count
    wide = tokens.astype(jnp.float32)
    squares = lax.psum(jnp.sum(wide * wide, axis=1, keepdims=True), "tensor")
    dma = pltpu.SemaphoreType.DMA
    vmem = pl.BlockSpec(memory_space=pltpu.VMEM)
    hbm = pl.BlockSpec(memory_space=pl.ANY)
    proj, pair = pl.pallas_call(
        functools.partial(gather_kernel, m),
        out_shape=(
            jax.ShapeDtypeStruct((3, rows, width), jnp.float32),
            jax.ShapeDtypeStruct((m, 2 * width, width), jnp.bfloat16),
        ),
        in_specs=[vmem, vmem, hbm, hbm],
        out_specs=(vmem, hbm),
        scratch_shapes=[
            pltpu.VMEM((m, 2, rows, width), jnp.bfloat16),
            pltpu.VMEM((3, depth, width), jnp.bfloat16),
            dma((m,)),
            dma((m - 1, 2, PIECES)),
            dma((m - 1, 2, PIECES)),
            dma((m - 1, 2, PIECES)),
            dma((m - 1, 2, PIECES)),
            dma,
            dma,
            dma((m,)),
            dma((m,)),
            dma((m,)),
        ],
        compiler_params=pltpu.CompilerParams(
            collective_id=0, has_side_effects=True, vmem_limit_bytes=50 << 20
        ),
        cost_estimate=pl.CostEstimate(
            flops=2 * rows * depth * 3 * width,
            bytes_accessed=2 * depth * width * 5,
            transcendentals=0,
        ),
        name="gather_project",
    )(tokens, norm_gain[None, :], jnp.transpose(w_in, (1, 0, 2)), w_out)
    factor = lax.rsqrt(squares / depth + 1e-05)
    flipped = filters[:, ::-1].astype(jnp.float32)
    line = jnp.pad(flipped, ((0, 0), (1, taps - 1)))
    return pl.pallas_call(
        functools.partial(scatter_kernel, m, taps, group),
        out_shape=jax.ShapeDtypeStruct((rows, width), jnp.bfloat16),
        in_specs=[vmem, vmem, vmem, vmem, vmem, hbm, vmem],
        out_specs=vmem,
        scratch_shapes=[
            pltpu.VMEM((m, 2 * width, width), jnp.bfloat16),
            pltpu.VMEM((2, rows, width), jnp.bfloat16),
            pltpu.VMEM((rows + taps, LANES), jnp.bfloat16),
            pltpu.VMEM((LANES // group * taps, 2 * taps), jnp.bfloat16),
            pltpu.VMEM((2, m - 1, rows // 2, width), jnp.bfloat16),
            pltpu.VMEM((2, m - 1, rows // 2, width), jnp.bfloat16),
            dma,
            dma((m - 1, 2, PIECES)),
            dma((m - 1, 2, PIECES)),
            dma((width // LANES,)),
            dma((width // LANES,)),
        ],
        compiler_params=pltpu.CompilerParams(
            collective_id=1, has_side_effects=True, vmem_limit_bytes=40 << 20
        ),
        cost_estimate=pl.CostEstimate(
            flops=2 * rows * depth * width, bytes_accessed=2 * depth * width, transcendentals=0
        ),
        name="filter_scatter",
    )(proj, factor, w_short, line, skip[None, :], pair, tokens)


def solution(mesh):
    return jax.shard_map(
        functools.partial(on_device, mesh.shape["tensor"]),
        mesh=mesh,
        in_specs=(
            P("groups", "tensor"),
            P("tensor"),
            P(None, None, "tensor"),
            P(None, None, "tensor"),
            P("tensor", None),
            P("tensor"),
            P("tensor", None),
        ),
        out_specs=P("groups", "tensor"),
        check_vma=False,
    )
```

```python
import functools

import jax
import jax.numpy as jnp
from jax import lax
from jax.experimental import pallas as pl
from jax.experimental.pallas import tpu as pltpu
from jax.sharding import PartitionSpec as P

MESH = pl.DeviceIdType.MESH
LANES = 128
PIECES = 2
HIGHEST = lax.Precision.HIGHEST


def chip_at(pos, m):
    upper = pos // (m // 2)
    return (1 - upper) * 2 * pos + upper * (2 * (m - 1 - pos) + 1)


def position_of(chip, m):
    odd = chip % 2
    return (1 - odd) * (chip // 2) + odd * (m - 1 - chip // 2)


class Ring:
    def __init__(self, m):
        me = lax.axis_index("tensor")
        self.m = m
        self.core = me % 2
        self.chip = me // 2
        self.pos = position_of(self.chip, m)
        self.next = (
            {"tensor": chip_at((self.pos + 1) % m, m) * 2 + self.core},
            {"tensor": chip_at((self.pos + m - 1) % m, m) * 2 + self.core},
        )
        self.sibling = {"tensor": self.chip * 2 + 1 - self.core}

    def behind(self, side, steps):
        if side == 0:
            return (self.pos + self.m - steps) % self.m
        return (self.pos + steps) % self.m

    def greet(self):
        barrier = pltpu.get_barrier_semaphore()
        for device in self.next + (self.sibling,):
            pl.semaphore_signal(barrier, inc=1, device_id=device, device_id_type=MESH)

    def met(self):
        pl.semaphore_wait(pltpu.get_barrier_semaphore(), 3)


def remote(src, dst, send, recv, device):
    return pltpu.make_async_remote_copy(
        src_ref=src, dst_ref=dst, send_sem=send, recv_sem=recv,
        device_id=device, device_id_type=MESH,
    )


def block_kernel(
    m, taps, group, tokens, gain, w_short, line, skip, w_in, w_out, out,
    xg, sums, wv, wo, acc, hid, gs, toep, stage, got,
    w_sem, ring_send, ring_recv, sib_send, sib_recv, own_send, own_recv,
    keep_sem, give_send, give_recv, rs_send, rs_recv, hid_send, hid_recv,
):
    rows, width = tokens.shape
    half = rows // 2
    piece = half // PIECES
    window = 2 * taps
    per_tile = LANES // group
    tiles = width // LANES
    ring = Ring(m)
    core = ring.core
    ring.greet()

    def w_copy(d):
        base = pl.multiple_of(chip_at((ring.pos + d) % m, m) * 2 * width, 2 * width)
        part = pl.ds(base, 2 * width)
        return pltpu.make_async_copy(w_in.at[:, part, :], wv.at[:, part, :], w_sem.at[d])

    w_copy(0).start()
    wide = tokens[...].astype(jnp.float32)
    xg[ring.pos, core] = (wide * gain[...]).astype(jnp.bfloat16)
    ring.met()

    def view(side, k, q, c):
        if k < PIECES:
            return xg.at[q, c, pl.ds(side * half + k * piece, piece), :]
        return sums.at[q, c, side]

    def hop(s, side, k, q):
        block = view(side, k, q, core)
        return remote(block, block, ring_send.at[s, side, k], ring_recv.at[s, side, k], ring.next[side])

    def across(s, side, k, q, c):
        block = view(side, k, q, c)
        return remote(block, block, sib_send.at[s, side, k], sib_recv.at[s, side, k], ring.sibling)

    parts = [(side, k) for k in range(PIECES) for side in range(2)]
    extra = [(side, PIECES) for side in range(2)]
    every_part = parts + extra
    for side, k in parts:
        hop(0, side, k, ring.pos).start()

    def own(c):
        block = xg.at[ring.pos, c]
        return remote(block, block, own_send.at[0], own_recv.at[0], ring.sibling)

    def own_sums(c):
        block = sums.at[ring.pos, c]
        return remote(block, block, own_send.at[1], own_recv.at[1], ring.sibling)

    own(core).start()
    ones = jnp.ones((8, width), jnp.float32)
    for side in range(2):
        mine = wide[side * half : (side + 1) * half]
        sums[ring.pos, core, side] = lax.dot_general(
            ones, mine * mine, (((1,), (1,)), ((), ())),
            precision=HIGHEST, preferred_element_type=jnp.float32,
        )
        hop(0, side, PIECES, ring.pos).start()
    own_sums(core).start()
    for d in range(1, m // 2 + 1):
        w_copy(d).start()
        if d < m - d:
            w_copy(m - d).start()

    def keep(q):
        base = pl.multiple_of((chip_at(q, m) * 2 + core) * width, width)
        return pltpu.make_async_copy(w_out.at[:, pl.ds(base, width)], wo.at[q, core], keep_sem.at[q])

    def give(q):
        base = pl.multiple_of((chip_at(q, m) * 2 + 1 - core) * width, width)
        return remote(
            w_out.at[:, pl.ds(base, width)], wo.at[q, core], give_send.at[q], give_recv.at[q], ring.sibling
        )

    def multiply(s, first):
        for side in range(2):
            q = ring.behind(side, s)
            here = pl.ds(side * half, half)
            base = pl.multiple_of(chip_at(q, m) * 2 * width, 2 * width)
            for b in range(3):
                term = jnp.dot(
                    xg[q, 0, here, :], wv[b, pl.ds(base, width), :],
                    preferred_element_type=jnp.float32,
                ) + jnp.dot(
                    xg[q, 1, here, :], wv[b, pl.ds(base + width, width), :],
                    preferred_element_type=jnp.float32,
                )
                if first:
                    acc[b, here, :] = term
                else:
                    acc[b, here, :] += term

    def pass_on(s, last):
        for side, k in every_part:
            q = ring.behind(side, s + 1)
            hop(s, side, k, q).wait_recv()
            if not last:
                hop(s + 1, side, k, q).start()
            across(s, side, k, q, core).start()

    def use(s):
        @pl.when(s <= m // 2)
        def _():
            w_copy(s).wait()

        @pl.when(s < m // 2)
        def _():
            w_copy(m - s).wait()

        for side, k in every_part:
            across(s - 1, side, k, ring.behind(side, s), 1 - core).wait_recv()
        multiply(s, False)

    def build(j, carry):
        lines = line[pl.ds(pl.multiple_of(j * per_tile, per_tile), per_tile), :]
        for f in range(per_tile):
            spread = jnp.broadcast_to(lines[f : f + 1, :], (taps, window))
            toep[j, f * taps : (f + 1) * taps, :] = pltpu.roll(
                spread, 0, 1, stride=1, stride_axis=0
            ).astype(jnp.bfloat16)
        return carry

    gs[0:taps, :] = jnp.zeros((taps, LANES), jnp.bfloat16)
    lax.fori_loop(0, tiles, build, 0)
    w_copy(0).wait()
    own(1 - core).wait_recv()
    own_sums(1 - core).wait_recv()
    multiply(0, True)
    pass_on(0, m == 2)

    def gather_step(s, carry):
        keep(s - 1).start()
        give(s - 1).start()
        use(s)
        pass_on(s, False)
        return carry

    lax.fori_loop(1, m - 2, gather_step, 0)
    for q in range(m - 3, m):
        keep(q).start()
        give(q).start()
    use(m - 2)
    pass_on(m - 2, True)
    use(m - 1)

    def total(q, carry):
        return carry + (sums[q, 0] + sums[q, 1])

    squares = lax.fori_loop(0, m, total, jnp.zeros((2, 8, half), jnp.float32))
    factors = lax.rsqrt(squares / w_in.shape[1] + 1e-05)
    factor = jnp.concatenate([factors[0].T[:, 0:1], factors[1].T[:, 0:1]], axis=0)

    def tell(j, c):
        block = hid.at[c, :, pl.ds(pl.multiple_of(j * LANES, LANES), LANES)]
        return remote(block, block, hid_send.at[j], hid_recv.at[j], ring.sibling)

    def tile(j, carry):
        lanes = pl.ds(pl.multiple_of(j * LANES, LANES), LANES)
        at_row = lax.broadcasted_iota(jnp.int32, (rows, LANES), 0)

        def short(b):
            x = acc[b, :, lanes] * factor
            result = w_short[0, pl.ds(b, 1), lanes] * x
            for lag in range(1, w_short.shape[0]):
                moved = jnp.where(at_row >= lag, pltpu.roll(x, lag, 0), 0.0)
                result = result + w_short[lag, pl.ds(b, 1), lanes] * moved
            return result

        gs[taps:, :] = (short(1) * short(2)).astype(jnp.bfloat16)
        query = short(0)
        owner = lax.broadcasted_iota(jnp.int32, (taps, LANES), 1) // group
        for i in range(rows // taps):
            every = jnp.dot(
                toep[j], gs[i * taps : i * taps + window, :], preferred_element_type=jnp.float32
            )
            conv = every[0:taps]
            for f in range(1, per_tile):
                conv = jnp.where(owner == f, every[f * taps : (f + 1) * taps], conv)
            gated = gs[(i + 1) * taps : (i + 2) * taps, :].astype(jnp.float32)
            part = (conv + skip[:, lanes] * gated) * query[i * taps : (i + 1) * taps]
            hid[core, i * taps : (i + 1) * taps, lanes] = part.astype(jnp.bfloat16)
        tell(j, core).start()
        return carry

    lax.fori_loop(0, tiles, tile, 0)

    def arrived(q, carry):
        keep(q).wait()
        block = wo.at[q, 1 - core]
        remote(block, block, give_send.at[q], give_recv.at[q], ring.sibling).wait_recv()
        return carry

    lax.fori_loop(0, m, arrived, 0)
    for j in range(tiles):
        tell(j, 1 - core).wait_recv()

    def span(k):
        return pl.ds(k * piece, piece)

    def reduce_hop(s, side, k):
        return remote(
            stage.at[side, s, span(k), :], got.at[side, s, span(k), :],
            rs_send.at[s, side, k], rs_recv.at[s, side, k], ring.next[side],
        )

    def partial(side, k, q):
        here = pl.ds(side * half + k * piece, piece)
        return jnp.dot(
            hid[0, here, :], wo[q, 0], preferred_element_type=jnp.float32
        ) + jnp.dot(
            hid[1, here, :], wo[q, 1], preferred_element_type=jnp.float32
        )

    for side, k in parts:
        stage[side, 0, span(k), :] = partial(side, k, ring.behind(side, 1)).astype(jnp.bfloat16)
        reduce_hop(0, side, k).start()

    def reduce_step(s, carry):
        for side, k in parts:
            part = partial(side, k, ring.behind(side, s + 1))
            reduce_hop(s - 1, side, k).wait_recv()
            part = part + got[side, s - 1, span(k), :].astype(jnp.float32)
            stage[side, s, span(k), :] = part.astype(jnp.bfloat16)
            reduce_hop(s, side, k).start()
        return carry

    lax.fori_loop(1, m - 1, reduce_step, 0)
    for side, k in parts:
        here = pl.ds(side * half + k * piece, piece)
        part = tokens[here, :].astype(jnp.float32) + partial(side, k, ring.pos)
        reduce_hop(m - 2, side, k).wait_recv()
        part = part + got[side, m - 2, span(k), :].astype(jnp.float32)
        out[here, :] = part.astype(jnp.bfloat16)

    own(core).wait_send()
    own_sums(core).wait_send()

    def settle(s, carry):
        for side, k in every_part:
            hop(s, side, k, ring.behind(side, s)).wait_send()
            across(s, side, k, ring.behind(side, s + 1), core).wait_send()
        for side, k in parts:
            reduce_hop(s, side, k).wait_send()
        return carry

    lax.fori_loop(0, m - 1, settle, 0)

    def given(q, carry):
        give(q).wait_send()
        return carry

    lax.fori_loop(0, m, given, 0)
    for j in range(tiles):
        tell(j, core).wait_send()


def on_device(n, tokens, norm_gain, w_in, w_short, filters, skip, w_out):
    m = n // 2
    rows, width = tokens.shape
    depth = w_in.shape[0]
    count, taps = filters.shape
    group = width // count
    flipped = filters[:, ::-1].astype(jnp.float32)
    line = jnp.pad(flipped, ((0, 0), (1, taps - 1)))
    dma = pltpu.SemaphoreType.DMA
    vmem = pl.BlockSpec(memory_space=pltpu.VMEM)
    hbm = pl.BlockSpec(memory_space=pl.ANY)
    return pl.pallas_call(
        functools.partial(block_kernel, m, taps, group),
        out_shape=jax.ShapeDtypeStruct((rows, width), jnp.bfloat16),
        in_specs=[vmem, vmem, vmem, vmem, vmem, hbm, hbm],
        out_specs=vmem,
        scratch_shapes=[
            pltpu.VMEM((m, 2, rows, width), jnp.bfloat16),
            pltpu.VMEM((m, 2, 2, 8, rows // 2), jnp.float32),
            pltpu.VMEM((3, depth, width), jnp.bfloat16),
            pltpu.VMEM((m, 2, width, width), jnp.bfloat16),
            pltpu.VMEM((3, rows, width), jnp.float32),
            pltpu.VMEM((2, rows, width), jnp.bfloat16),
            pltpu.VMEM((rows + taps, LANES), jnp.bfloat16),
            pltpu.VMEM((width // LANES, LANES // group * taps, 2 * taps), jnp.bfloat16),
            pltpu.VMEM((2, m - 1, rows // 2, width), jnp.bfloat16),
            pltpu.VMEM((2, m - 1, rows // 2, width), jnp.bfloat16),
            dma((m,)),
            dma((m - 1, 2, PIECES + 1)),
            dma((m - 1, 2, PIECES + 1)),
            dma((m - 1, 2, PIECES + 1)),
            dma((m - 1, 2, PIECES + 1)),
            dma((2,)),
            dma((2,)),
            dma((m,)),
            dma((m,)),
            dma((m,)),
            dma((m - 1, 2, PIECES)),
            dma((m - 1, 2, PIECES)),
            dma((width // LANES,)),
            dma((width // LANES,)),
        ],
        compiler_params=pltpu.CompilerParams(
            collective_id=0, has_side_effects=True, vmem_limit_bytes=58 << 20
        ),
        name="hyena_block",
    )(tokens, norm_gain[None, :], w_short, line, skip[None, :], jnp.transpose(w_in, (1, 0, 2)), w_out)


def solution(mesh):
    return jax.shard_map(
        functools.partial(on_device, mesh.shape["tensor"]),
        mesh=mesh,
        in_specs=(
            P("groups", "tensor"),
            P("tensor"),
            P(None, None, "tensor"),
            P(None, None, "tensor"),
            P("tensor", None),
            P("tensor"),
            P("tensor", None),
        ),
        out_specs=P("groups", "tensor"),
        check_vma=False,
    )
```

```python
import functools

import jax
import jax.numpy as jnp
from jax import lax
from jax.experimental import pallas as pl
from jax.experimental.pallas import tpu as pltpu
from jax.sharding import PartitionSpec as P

MESH = pl.DeviceIdType.MESH
LANES = 128
PIECES = 2
HIGHEST = lax.Precision.HIGHEST


def chip_at(pos, m):
    upper = pos // (m // 2)
    return (1 - upper) * 2 * pos + upper * (2 * (m - 1 - pos) + 1)


def position_of(chip, m):
    odd = chip % 2
    return (1 - odd) * (chip // 2) + odd * (m - 1 - chip // 2)


class Ring:
    def __init__(self, m):
        me = lax.axis_index("tensor")
        self.m = m
        self.core = me % 2
        self.chip = me // 2
        self.pos = position_of(self.chip, m)
        self.next = (
            {"tensor": chip_at((self.pos + 1) % m, m) * 2 + self.core},
            {"tensor": chip_at((self.pos + m - 1) % m, m) * 2 + self.core},
        )
        self.sibling = {"tensor": self.chip * 2 + 1 - self.core}

    def behind(self, side, steps):
        if side == 0:
            return (self.pos + self.m - steps) % self.m
        return (self.pos + steps) % self.m

    def greet(self):
        barrier = pltpu.get_barrier_semaphore()
        for device in self.next + (self.sibling,):
            pl.semaphore_signal(barrier, inc=1, device_id=device, device_id_type=MESH)

    def met(self):
        pl.semaphore_wait(pltpu.get_barrier_semaphore(), 3)


def remote(src, dst, send, recv, device):
    return pltpu.make_async_remote_copy(
        src_ref=src, dst_ref=dst, send_sem=send, recv_sem=recv,
        device_id=device, device_id_type=MESH,
    )


def block_kernel(
    m, taps, group, tokens, gain, w_short, filters, skip, w_in, w_out, out,
    xg, sums, wv, wo, acc, hid, gs, toep, stage, got, line, tail,
    w_sem, ring_send, ring_recv, sib_send, sib_recv, own_send, own_recv,
    keep_sem, give_send, give_recv, rs_send, rs_recv, hid_send, hid_recv,
):
    rows, width = tokens.shape
    half = rows // 2
    piece = half // PIECES
    window = 2 * taps
    per_tile = LANES // group
    tiles = width // LANES
    ring = Ring(m)
    core = ring.core
    ring.greet()

    def w_copy(d):
        base = pl.multiple_of(chip_at((ring.pos + d) % m, m) * 2 * width, 2 * width)
        part = pl.ds(base, 2 * width)
        return pltpu.make_async_copy(w_in.at[:, part, :], wv.at[:, part, :], w_sem.at[d])

    w_copy(0).start()
    wide = tokens[...].astype(jnp.float32)
    scaled = (wide * gain[...]).astype(jnp.bfloat16)
    for k in range(PIECES):
        for side in range(2):
            first = (k * 2 + side) * piece
            xg[ring.pos, core, pl.ds(side * half + k * piece, piece), :] = scaled[first : first + piece]
    ring.met()

    def view(side, k, q, c):
        if k < PIECES:
            return xg.at[q, c, pl.ds(side * half + k * piece, piece), :]
        return sums.at[q, c, side]

    def hop(s, side, k, q):
        block = view(side, k, q, core)
        return remote(block, block, ring_send.at[s, side, k], ring_recv.at[s, side, k], ring.next[side])

    def across(s, side, k, q, c):
        block = view(side, k, q, c)
        return remote(block, block, sib_send.at[s, side, k], sib_recv.at[s, side, k], ring.sibling)

    parts = [(side, k) for k in range(PIECES) for side in range(2)]
    extra = [(side, PIECES) for side in range(2)]
    every_part = extra + parts
    for side, k in parts:
        hop(0, side, k, ring.pos).start()

    def own(c):
        block = xg.at[ring.pos, c]
        return remote(block, block, own_send.at[0], own_recv.at[0], ring.sibling)

    def own_sums(c):
        block = sums.at[ring.pos, c]
        return remote(block, block, own_send.at[1], own_recv.at[1], ring.sibling)

    own(core).start()
    ones = jnp.ones((8, width), jnp.float32)
    for side in range(2):
        mine = jnp.concatenate(
            [wide[(k * 2 + side) * piece : (k * 2 + side + 1) * piece] for k in range(PIECES)], axis=0
        )
        sums[ring.pos, core, side] = lax.dot_general(
            ones, mine * mine, (((1,), (1,)), ((), ())),
            precision=HIGHEST, preferred_element_type=jnp.float32,
        )
        hop(0, side, PIECES, ring.pos).start()
    own_sums(core).start()
    for d in range(1, m // 2 + 1):
        w_copy(d).start()
        if d < m - d:
            w_copy(m - d).start()

    def keep(q):
        base = pl.multiple_of((chip_at(q, m) * 2 + core) * width, width)
        return pltpu.make_async_copy(w_out.at[:, pl.ds(base, width)], wo.at[q, core], keep_sem.at[q])

    def give(q):
        base = pl.multiple_of((chip_at(q, m) * 2 + 1 - core) * width, width)
        return remote(
            w_out.at[:, pl.ds(base, width)], wo.at[q, core], give_send.at[q], give_recv.at[q], ring.sibling
        )

    def multiply(s, first):
        for side in range(2):
            q = ring.behind(side, s)
            here = pl.ds(side * half, half)
            base = pl.multiple_of(chip_at(q, m) * 2 * width, 2 * width)
            for b in range(3):
                term = jnp.dot(
                    xg[q, 0, here, :], wv[b, pl.ds(base, width), :],
                    preferred_element_type=jnp.float32,
                ) + jnp.dot(
                    xg[q, 1, here, :], wv[b, pl.ds(base + width, width), :],
                    preferred_element_type=jnp.float32,
                )
                if first:
                    acc[b, here, :] = term
                else:
                    acc[b, here, :] += term

    def multiply_piece(s, k):
        for side in range(2):
            q = ring.behind(side, s)
            here = pl.ds(side * half + k * piece, piece)
            base = pl.multiple_of(chip_at(q, m) * 2 * width, 2 * width)
            for b in range(3):
                acc[b, here, :] += jnp.dot(
                    xg[q, 0, here, :], wv[b, pl.ds(base, width), :],
                    preferred_element_type=jnp.float32,
                ) + jnp.dot(
                    xg[q, 1, here, :], wv[b, pl.ds(base + width, width), :],
                    preferred_element_type=jnp.float32,
                )

    def pass_on(s, last, chosen=every_part):
        for side, k in chosen:
            q = ring.behind(side, s + 1)
            hop(s, side, k, q).wait_recv()
            if not last:
                hop(s + 1, side, k, q).start()
            across(s, side, k, q, core).start()

    def use(s):
        @pl.when(s <= m // 2)
        def _():
            w_copy(s).wait()

        @pl.when(s < m // 2)
        def _():
            w_copy(m - s).wait()

        for side, k in every_part:
            across(s - 1, side, k, ring.behind(side, s), 1 - core).wait_recv()
        multiply(s, False)

    def build(j, carry):
        lines = line[pl.ds(pl.multiple_of(j * per_tile, per_tile), per_tile), :]
        for f in range(per_tile):
            spread = jnp.broadcast_to(lines[f : f + 1, :], (taps, window))
            toep[j, f * taps : (f + 1) * taps, :] = pltpu.roll(
                spread, 0, 1, stride=1, stride_axis=0
            ).astype(jnp.bfloat16)
        return carry

    place = lax.broadcasted_iota(jnp.int32, (taps, taps), 0) + lax.broadcasted_iota(jnp.int32, (taps, taps), 1)
    for side, where in ((0, taps), (1, 0)):
        line[:, side * taps : (side + 1) * taps] = jnp.dot(
            filters[...], jnp.where(place == where, 1.0, 0.0).astype(jnp.bfloat16),
            preferred_element_type=jnp.float32,
        )
    gs[0:taps, :] = jnp.zeros((taps, width), jnp.bfloat16)
    lax.fori_loop(0, tiles, build, 0)
    w_copy(0).wait()
    own(1 - core).wait_recv()
    own_sums(1 - core).wait_recv()
    multiply(0, True)
    pass_on(0, m == 2)

    def gather_step(s, carry):
        keep(s - 1).start()
        give(s - 1).start()
        use(s)
        pass_on(s, False)
        return carry

    lax.fori_loop(1, m - 2, gather_step, 0)
    for q in range(m - 3, m):
        keep(q).start()
        give(q).start()
    use(m - 2)
    def landed(s, chosen):
        for side, k in chosen:
            across(s, side, k, ring.behind(side, s + 1), 1 - core).wait_recv()

    def at_piece(k):
        return [(0, k), (1, k)]

    pass_on(m - 2, True, extra + at_piece(0))
    landed(m - 2, extra)

    def total(q, carry):
        return carry + (sums[q, 0] + sums[q, 1])

    squares = lax.fori_loop(0, m, total, jnp.zeros((2, 8, half), jnp.float32))
    factors = lax.rsqrt(squares / w_in.shape[1] + 1e-05)
    factor = [factors[side].T[:, 0:1] for side in range(2)]
    both = 2 * piece

    def tell(k, j, c):
        block = hid.at[c, pl.ds(k * both, both), pl.ds(pl.multiple_of(j * LANES, LANES), LANES)]
        return remote(block, block, hid_send.at[k, j], hid_recv.at[k, j], ring.sibling)

    def tile(k, j, carry):
        lanes = pl.ds(pl.multiple_of(j * LANES, LANES), LANES)

        def short(b):
            blocks = [
                acc[b, side * half + k * piece : side * half + (k + 1) * piece, lanes]
                * factor[side][k * piece : (k + 1) * piece]
                for side in range(2)
            ]
            before = jnp.zeros((8, LANES), jnp.float32) if k == 0 else tail[b, :, lanes]
            x = jnp.concatenate([before] + blocks, axis=0)
            tail[b, :, lanes] = x[both:]
            result = w_short[0, pl.ds(b, 1), lanes] * x[8:]
            for lag in range(1, w_short.shape[0]):
                result = result + w_short[lag, pl.ds(b, 1), lanes] * pltpu.roll(x, lag, 0)[8:]
            return result

        gs[taps + k * both : taps + (k + 1) * both, lanes] = (short(1) * short(2)).astype(jnp.bfloat16)
        query = short(0)
        owner = lax.broadcasted_iota(jnp.int32, (taps, LANES), 1) // group
        for i in range(both // taps):
            start = k * both + i * taps
            every = jnp.dot(
                toep[j], gs[start : start + window, lanes], preferred_element_type=jnp.float32
            )
            conv = every[0:taps]
            for f in range(1, per_tile):
                conv = jnp.where(owner == f, every[f * taps : (f + 1) * taps], conv)
            gated = gs[start + taps : start + window, lanes].astype(jnp.float32)
            part = (conv + skip[:, lanes] * gated) * query[i * taps : (i + 1) * taps]
            hid[core, start : start + taps, lanes] = part.astype(jnp.bfloat16)
        tell(k, j, core).start()
        return carry

    def arrived(q, carry):
        keep(q).wait()
        block = wo.at[q, 1 - core]
        remote(block, block, give_send.at[q], give_recv.at[q], ring.sibling).wait_recv()
        return carry


    def span(k):
        return pl.ds(k * piece, piece)

    def reduce_hop(s, side, k):
        return remote(
            stage.at[side, s, span(k), :], got.at[side, s, span(k), :],
            rs_send.at[s, side, k], rs_recv.at[s, side, k], ring.next[side],
        )

    def partial(side, k, q):
        here = pl.ds((k * 2 + side) * piece, piece)
        return jnp.dot(
            hid[0, here, :], wo[q, 0], preferred_element_type=jnp.float32
        ) + jnp.dot(
            hid[1, here, :], wo[q, 1], preferred_element_type=jnp.float32
        )

    for k in range(PIECES):
        landed(m - 2, at_piece(k))
        multiply_piece(m - 1, k)
        if k + 1 < PIECES:
            pass_on(m - 2, True, at_piece(k + 1))
        lax.fori_loop(0, tiles, functools.partial(tile, k), 0)
        if k == 0:
            lax.fori_loop(0, m, arrived, 0)
        for j in range(tiles):
            tell(k, j, 1 - core).wait_recv()
        for side in range(2):
            stage[side, 0, span(k), :] = partial(side, k, ring.behind(side, 1)).astype(jnp.bfloat16)
            reduce_hop(0, side, k).start()

    def reduce_step(s, carry):
        for side, k in parts:
            part = partial(side, k, ring.behind(side, s + 1))
            reduce_hop(s - 1, side, k).wait_recv()
            part = part + got[side, s - 1, span(k), :].astype(jnp.float32)
            stage[side, s, span(k), :] = part.astype(jnp.bfloat16)
            reduce_hop(s, side, k).start()
        return carry

    lax.fori_loop(1, m - 1, reduce_step, 0)
    for side, k in parts:
        here = pl.ds((k * 2 + side) * piece, piece)
        part = tokens[here, :].astype(jnp.float32) + partial(side, k, ring.pos)
        reduce_hop(m - 2, side, k).wait_recv()
        part = part + got[side, m - 2, span(k), :].astype(jnp.float32)
        out[here, :] = part.astype(jnp.bfloat16)

    own(core).wait_send()
    own_sums(core).wait_send()

    def settle(s, carry):
        for side, k in every_part:
            hop(s, side, k, ring.behind(side, s)).wait_send()
            across(s, side, k, ring.behind(side, s + 1), core).wait_send()
        for side, k in parts:
            reduce_hop(s, side, k).wait_send()
        return carry

    lax.fori_loop(0, m - 1, settle, 0)

    def given(q, carry):
        give(q).wait_send()
        return carry

    lax.fori_loop(0, m, given, 0)
    for k in range(PIECES):
        for j in range(tiles):
            tell(k, j, core).wait_send()


def on_device(n, tokens, norm_gain, w_in, w_short, filters, skip, w_out):
    m = n // 2
    rows, width = tokens.shape
    depth = w_in.shape[0]
    count, taps = filters.shape
    group = width // count
    dma = pltpu.SemaphoreType.DMA
    vmem = pl.BlockSpec(memory_space=pltpu.VMEM)
    hbm = pl.BlockSpec(memory_space=pl.ANY)
    return pl.pallas_call(
        functools.partial(block_kernel, m, taps, group),
        out_shape=jax.ShapeDtypeStruct((rows, width), jnp.bfloat16),
        in_specs=[vmem, vmem, vmem, vmem, vmem, hbm, hbm],
        out_specs=vmem,
        scratch_shapes=[
            pltpu.VMEM((m, 2, rows, width), jnp.bfloat16),
            pltpu.VMEM((m, 2, 2, 8, rows // 2), jnp.float32),
            pltpu.VMEM((3, depth, width), jnp.bfloat16),
            pltpu.VMEM((m, 2, width, width), jnp.bfloat16),
            pltpu.VMEM((3, rows, width), jnp.float32),
            pltpu.VMEM((2, rows, width), jnp.bfloat16),
            pltpu.VMEM((rows + taps, width), jnp.bfloat16),
            pltpu.VMEM((width // LANES, LANES // group * taps, 2 * taps), jnp.bfloat16),
            pltpu.VMEM((2, m - 1, rows // 2, width), jnp.bfloat16),
            pltpu.VMEM((2, m - 1, rows // 2, width), jnp.bfloat16),
            pltpu.VMEM((count, 2 * taps), jnp.float32),
            pltpu.VMEM((3, 8, width), jnp.float32),
            dma((m,)),
            dma((m - 1, 2, PIECES + 1)),
            dma((m - 1, 2, PIECES + 1)),
            dma((m - 1, 2, PIECES + 1)),
            dma((m - 1, 2, PIECES + 1)),
            dma((2,)),
            dma((2,)),
            dma((m,)),
            dma((m,)),
            dma((m,)),
            dma((m - 1, 2, PIECES)),
            dma((m - 1, 2, PIECES)),
            dma((PIECES, width // LANES)),
            dma((PIECES, width // LANES)),
        ],
        compiler_params=pltpu.CompilerParams(
            collective_id=0, has_side_effects=True, vmem_limit_bytes=58 << 20
        ),
        name="hyena_block",
    )(tokens, norm_gain[None, :], w_short, filters, skip[None, :], jnp.transpose(w_in, (1, 0, 2)), w_out)


def solution(mesh):
    return jax.shard_map(
        functools.partial(on_device, mesh.shape["tensor"]),
        mesh=mesh,
        in_specs=(
            P("groups", "tensor"),
            P("tensor"),
            P(None, None, "tensor"),
            P(None, None, "tensor"),
            P("tensor", None),
            P("tensor"),
            P("tensor", None),
        ),
        out_specs=P("groups", "tensor"),
        check_vma=False,
    )
```
